512 devices in a mesh: dp: 64 (over y, z), mp: 8 (over x, core).
Axes of the slice: x: 4, y: 4, z: 16, core: 2. Of those that a mesh axis runs over, the one named last changes fastest.
Arguments:
- tokens_in: bfloat16 [8192, 8192], P('dp', 'mp'), may hold values from -6 to 6
- gate_pre: bfloat16 [8192, 28672], P('dp', 'mp'), may hold values from -8 to 8
- up_pre: bfloat16 [8192, 28672], P('dp', 'mp'), may hold values from -6 to 6
- hidden_grad: bfloat16 [8192, 28672], P('dp', 'mp'), may hold values from -160 to 160
- out_grad: bfloat16 [8192, 8192], P('dp', 'mp'), may hold values from -160 to 160
- proj_model: bfloat16 [8192, 128], P('mp'), may hold values from -0.0625 to 0.0625
- proj_hidden: bfloat16 [28672, 128], P('mp'), may hold values from -0.03125 to 0.03125
Outputs:
- whitened: float32 [64, 128, 64], P('dp', 'mp')
The draws below stay inside these ranges and needn't reach their ends.
All inputs are finite; a program needn't handle non-finite values.
Results may differ from the reference program's by a relative error of at most 0.003.
Values sent between devices are 32-bit elements; how exact they have to be, the bound alone decides.
A program may use at most 64 MiB of HBM per device.

```python
import math
import jax
import jax.numpy as jnp
from jax import lax

D = 8192
FF = 28672
RANK = 64
LEN = 128
EXAMPLES = 64
TOKENS = 8192


def example_scale(key, rising):
    scale_key = jax.random.fold_in(key, 11)
    position = jnp.arange(EXAMPLES, dtype=jnp.float32) / max(EXAMPLES - 1, 1)
    spread = jnp.exp(jax.random.uniform(scale_key, (EXAMPLES,), jnp.float32, 0.0, math.log(10.0)))
    return rising ** position * spread


def scaled_rows(key, columns_all):
    base_key = jax.random.fold_in(key, 3)
    base = jnp.clip(jax.random.normal(base_key, (TOKENS, columns_all), jnp.float32), -4.0, 4.0)
    rising = 3.0
    factors = jnp.repeat(example_scale(key, rising), LEN)
    return (base * factors[:, None]).astype(jnp.bfloat16)


def draw_hidden_grad(key, part):
    return scaled_rows(jax.random.fold_in(key, 101), FF)


def draw_out_grad(key, part):
    return scaled_rows(jax.random.fold_in(key, 202), D)


def block_levels(key, shape, split, smallest, high):
    def one(dim, parts):
        heights = jax.random.uniform(jax.random.fold_in(jax.random.fold_in(key, 6), dim), (parts,), jnp.float32, smallest / len(split), high / len(split))
        return jnp.repeat(jnp.exp(heights), shape[dim] // parts).reshape((-1,) + (1,) * (len(shape) - dim - 1))

    loudness = one(*split[0])
    for cut in split[1:]:
        loudness = loudness * one(*cut)
    return loudness


def centred(stream_key, shape, scale, most, split=(), kind=jnp.bfloat16):
    gain = block_levels(stream_key, shape, split, -0.22, 0.18) if split else 1.0
    values = jax.random.normal(stream_key, shape, jnp.float32) * scale * gain
    return jnp.minimum(jnp.maximum(values, -most), most).astype(kind)


def setup_inputs(seed: int = 0) -> dict:
    keys = jax.random.split(jax.random.key(seed), 8)
    return {
        "tokens_in": centred(keys[0], (TOKENS, D), 1.0, 6.0, ((0, 64), (1, 8))),
        "gate_pre": centred(keys[1], (TOKENS, FF), 1.5, 8.0, ((0, 64), (1, 8))),
        "up_pre": centred(keys[2], (TOKENS, FF), 1.0, 6.0, ((0, 64), (1, 8))),
        "hidden_grad": draw_hidden_grad(jax.random.fold_in(keys[7], 71), 0),
        "out_grad": draw_out_grad(jax.random.fold_in(keys[7], 71), 0),
        "proj_model": centred(keys[5], (D, 2 * RANK), D ** -0.5, 0.0625, ((0, 8),)),
        "proj_hidden": centred(keys[6], (FF, 2 * RANK), FF ** -0.5, 0.03125, ((0, 8),)),
    }


highest = lax.Precision.HIGHEST

def gradient_blocks(projected):
    columns_each = projected.shape[-1] // 4
    input_side = projected[..., :columns_each]
    output_side = projected[..., columns_each:2 * columns_each]
    upward = projected[..., 2 * columns_each:3 * columns_each]
    hidden_side = projected[..., 3 * columns_each:]
    up_block = jnp.einsum('elr,els->ers', input_side, upward, precision=highest)
    down_block = jnp.einsum('elr,els->ers', hidden_side, output_side, precision=highest)
    return jnp.concatenate([up_block, down_block], axis=1)

def reference(tokens_in, gate_pre, up_pre, hidden_grad, out_grad, proj_model, proj_hidden):

    def project(pieces):
        token_rows, gate_rows, up_rows, grad_rows, outer_rows = pieces
        gate_act = jax.nn.silu(gate_rows.astype(jnp.float32))
        up_grad = (grad_rows.astype(jnp.float32) * gate_act).astype(jnp.bfloat16)
        hidden = (gate_act * up_rows.astype(jnp.float32)).astype(jnp.bfloat16)
        projected = jnp.concatenate([jnp.dot(token_rows.astype(jnp.float32), proj_model[:, :RANK].astype(jnp.float32), preferred_element_type=jnp.float32), jnp.dot(outer_rows.astype(jnp.float32), proj_model[:, RANK:].astype(jnp.float32), preferred_element_type=jnp.float32), jnp.dot(up_grad.astype(jnp.float32), proj_hidden[:, :RANK].astype(jnp.float32), preferred_element_type=jnp.float32), jnp.dot(hidden.astype(jnp.float32), proj_hidden[:, RANK:].astype(jnp.float32), preferred_element_type=jnp.float32)], axis=1)
        return gradient_blocks(projected[None])[0]
    blocks = lax.map(project, (tokens_in.reshape(EXAMPLES, LEN, D), gate_pre.reshape(EXAMPLES, LEN, FF), up_pre.reshape(EXAMPLES, LEN, FF), hidden_grad.reshape(EXAMPLES, LEN, FF), out_grad.reshape(EXAMPLES, LEN, D)))
    flat_rows = blocks.reshape(EXAMPLES * 2 * RANK, RANK)
    gram = jnp.dot(flat_rows.T.astype(jnp.float32), flat_rows.astype(jnp.float32), precision=highest, preferred_element_type=jnp.float32)
    lower = jnp.linalg.cholesky(gram)
    solved = jax.scipy.linalg.solve_triangular(lower, flat_rows.T, lower=True)
    factor = math.sqrt(EXAMPLES * 2 * RANK)
    return (solved.T * factor).reshape(EXAMPLES, 2 * RANK, RANK)
```

```python
import functools
import math

import jax
import jax.numpy as jnp
from jax import lax
from jax.experimental import pallas as pl
from jax.experimental.pallas import tpu as pltpu
from jax.sharding import PartitionSpec as P

RANK = 64
LEN = 128
NY, NZ = 4, 16
NC = 2
CHUNK = 512
F32 = jnp.float32
BF16 = jnp.bfloat16
MESH = pl.DeviceIdType.MESH
NT = (((1,), (1,)), ((), ()))


def halves(value):
    high = value.astype(BF16)
    return high, (value - high.astype(F32)).astype(BF16)


def thirds(value):
    high = value.astype(BF16)
    rest = value - high.astype(F32)
    mid = rest.astype(BF16)
    return high, mid, (rest - mid.astype(F32)).astype(BF16)


def product_3(left, right):
    lh, ll = halves(left)
    rh, rl = halves(right)
    return lax.dot_general(
        jnp.concatenate([lh, lh, ll], axis=1),
        jnp.concatenate([rh, rl, rh], axis=1),
        NT,
        preferred_element_type=F32,
    )


def product_6(left, right):
    lh, lm, ll = thirds(left)
    rh, rm, rl = thirds(right)
    return lax.dot_general(
        jnp.concatenate([ll, lm, lh, lm, lh, lh], axis=1),
        jnp.concatenate([rh, rm, rl, rh, rm, rh], axis=1),
        NT,
        preferred_element_type=F32,
    )


def kernel(
    mp_size,
    tokens_hbm,
    gate_hbm,
    up_hbm,
    hidden_grad_hbm,
    out_grad_hbm,
    model_hbm,
    hidden_hbm,
    out_ref,
    tokens,
    gate,
    up,
    hidden_grad,
    out_grad,
    model,
    hidden,
    lhs,
    part,
    from_core,
    xbuf,
    sbuf,
    mbuf,
    packed,
    zbuf,
    fbuf,
    aug,
    rows_out,
    in_sem,
    chunk_sem,
    core_sem,
    x_sem,
    m_sem,
    z_sem,
    f_sem,
):
    nx = mp_size // NC
    dp = lax.axis_index("dp")
    mp = lax.axis_index("mp")
    y, z = dp // NZ, dp % NZ
    x, core = mp // NC, mp % NC
    chunks = gate.shape[0]

    first = [
        pltpu.make_async_copy(model_hbm, model, in_sem.at[0]),
        pltpu.make_async_copy(tokens_hbm, tokens, in_sem.at[1]),
        pltpu.make_async_copy(out_grad_hbm, out_grad, in_sem.at[2]),
    ]
    for copy in first:
        copy.start()
    later = []
    for i in range(chunks):
        span = pl.ds(i * CHUNK, CHUNK)
        group = [
            pltpu.make_async_copy(hidden_hbm.at[span, :], hidden.at[i], chunk_sem.at[i, 0]),
            pltpu.make_async_copy(gate_hbm.at[:, span], gate.at[i], chunk_sem.at[i, 1]),
            pltpu.make_async_copy(hidden_grad_hbm.at[:, span], hidden_grad.at[i], chunk_sem.at[i, 2]),
            pltpu.make_async_copy(up_hbm.at[:, span], up.at[i], chunk_sem.at[i, 3]),
        ]
        for copy in group:
            copy.start()
        later.append(group)

    barrier = pltpu.get_barrier_semaphore()
    plane = NY * mp_size

    def z_peer(apart):
        return (y * NZ + (z + apart) % NZ, mp)

    def plane_peer(apart):
        there = (y * mp_size + mp + apart) % plane
        return ((there // mp_size) * NZ + z, there % mp_size)

    def greet_z(apart, carry):
        pl.semaphore_signal(barrier, inc=1, device_id=z_peer(apart), device_id_type=MESH)
        return carry

    def greet_plane(apart, carry):
        pl.semaphore_signal(barrier, inc=1, device_id=plane_peer(apart), device_id_type=MESH)
        return carry

    lax.fori_loop(1, NZ, greet_z, 0)
    lax.fori_loop(1, plane, greet_plane, 0)

    for copy in first:
        copy.wait()
    from_model = jnp.dot(tokens[...], model[...], preferred_element_type=F32)
    from_model_out = jnp.dot(out_grad[...], model[...], preferred_element_type=F32)
    total = jnp.zeros((2 * LEN, 2 * RANK), F32)
    for i in range(chunks):
        for copy in later[i]:
            copy.wait()
        slot = i % 2
        for r in range(0, LEN, 32):
            block = pl.ds(r, 32)
            g = gate[i, block, :].astype(F32)
            half = 0.5 * g
            act = half + half * jnp.tanh(half)
            lhs[slot, block, :] = (hidden_grad[i, block, :].astype(F32) * act).astype(BF16)
            lhs[slot, pl.ds(LEN + r, 32), :] = (act * up[i, block, :].astype(F32)).astype(BF16)
        total = total + jnp.dot(lhs[slot], hidden[i], preferred_element_type=F32)
    lane = lax.broadcasted_iota(jnp.int32, (LEN, 2 * RANK), 1)
    low = lane < RANK
    part[0] = jnp.where(low, from_model, pltpu.roll(total[:LEN], RANK, 1))
    part[1] = jnp.where(low, pltpu.roll(from_model_out, RANK, 1), total[LEN:])

    pl.semaphore_wait(barrier, NZ - 1 + plane - 1)

    sibling = (dp, x * NC + 1 - core)
    swap = pltpu.make_async_remote_copy(
        part.at[1 - core], from_core, core_sem.at[0], core_sem.at[1], device_id=sibling, device_id_type=MESH
    )
    swap.start()
    swap.wait()
    xbuf[x] = part[core] + from_core[...]

    for apart in range(1, nx):
        pltpu.make_async_remote_copy(
            xbuf.at[x],
            xbuf.at[x],
            x_sem.at[0],
            x_sem.at[1],
            device_id=(dp, ((x + apart) % nx) * NC + core),
            device_id_type=MESH,
        ).start()
    all_x = pltpu.make_async_remote_copy(
        xbuf.at[pl.ds(0, nx - 1)],
        xbuf.at[pl.ds(0, nx - 1)],
        x_sem.at[0],
        x_sem.at[1],
        device_id=sibling,
        device_id_type=MESH,
    )
    all_x.wait_send()
    all_x.wait_recv()
    summed = xbuf[0]
    for i in range(1, nx):
        summed = summed + xbuf[i]

    turned = summed.T
    sbuf[...] = product_3(turned, turned)
    mine = pl.ds(pl.multiple_of((1 - core) * RANK, RANK), RANK)
    mbuf[core] = sbuf[mine, :]
    give = pltpu.make_async_remote_copy(
        mbuf.at[core], mbuf.at[core], m_sem.at[0], m_sem.at[1], device_id=sibling, device_id_type=MESH
    )
    give.start()
    give.wait()
    short_low = lax.broadcasted_iota(jnp.int32, (RANK, 2 * RANK), 1) < RANK
    stacked = jnp.where(short_low, mbuf[0], mbuf[1])

    gram = product_6(stacked, jnp.concatenate([stacked, stacked], axis=0))
    half_low = lax.broadcasted_iota(jnp.int32, (RANK // 2, 2 * RANK), 1) < RANK
    pairs = jnp.where(half_low, gram[: RANK // 2], gram[RANK // 2 :])
    size = packed.shape[1]
    for i in range(mp_size):
        packed[i] = pairs[i * size : (i + 1) * size]

    for apart in sorted(range(1, NZ), key=lambda d: -min(d, NZ - d)):
        pltpu.make_async_remote_copy(
            packed.at[mp], zbuf.at[z], z_sem.at[0], z_sem.at[1], device_id=z_peer(apart), device_id_type=MESH
        ).start()
    zbuf[z] = packed[mp]
    own = pltpu.roll(stacked, (RANK + 2 * RANK - mp * (2 * RANK // mp_size)) % (2 * RANK), 1)
    all_z = pltpu.make_async_remote_copy(
        zbuf.at[pl.ds(0, NZ - 1)],
        zbuf.at[pl.ds(0, NZ - 1)],
        z_sem.at[0],
        z_sem.at[1],
        device_id=sibling,
        device_id_type=MESH,
    )
    all_z.wait_send()
    all_z.wait_recv()
    slice_sum = zbuf[0]
    for i in range(1, NZ):
        slice_sum = slice_sum + zbuf[i]
    place = y * mp_size + mp
    fbuf[place] = slice_sum

    def send_plane(apart, carry):
        pltpu.make_async_remote_copy(
            fbuf.at[place], fbuf.at[place], f_sem.at[0], f_sem.at[1], device_id=plane_peer(apart), device_id_type=MESH
        ).start()
        return carry

    lax.fori_loop(1, plane, send_plane, 0)
    all_plane = pltpu.make_async_remote_copy(
        fbuf.at[pl.ds(0, plane - 1)],
        fbuf.at[pl.ds(0, plane - 1)],
        f_sem.at[0],
        f_sem.at[1],
        device_id=sibling,
        device_id_type=MESH,
    )
    all_plane.wait_send()
    all_plane.wait_recv()
    for i in range(mp_size):
        piece = fbuf[i]
        for j in range(1, NY):
            piece = piece + fbuf[j * mp_size + i]
        aug[i * size : (i + 1) * size, :] = piece
    folded = aug[...]
    whole = jnp.concatenate([folded, pltpu.roll(folded, RANK, 1)], axis=0)
    table = jnp.where(short_low, whole, own)

    tiles = [table[8 * i : 8 * i + 8] for i in range(RANK // 8)]
    for k in range(RANK):
        t, s = k // 8, k % 8
        row = jnp.broadcast_to(tiles[t][s : s + 1, :], (8, 2 * RANK))
        pivot = jnp.broadcast_to(row[:, k : k + 1], (8, 2 * RANK))
        rows_out[k : k + 1, :] = (row * lax.rsqrt(pivot))[:1]
        scaled = row / pivot
        for i in range(t, RANK // 8):
            column = jnp.broadcast_to(tiles[i][:, k : k + 1], (8, 2 * RANK))
            tiles[i] = tiles[i] - column * scaled
    factor = math.sqrt(NY * NZ * LEN)
    turned_out = rows_out[...].T
    out_ref[0] = turned_out[RANK : RANK + 2 * RANK // mp_size, :RANK] * factor


def shards(tokens_in, gate_pre, up_pre, hidden_grad, out_grad, proj_model, proj_hidden):
    mp_size = lax.axis_size("mp")
    length, width = tokens_in.shape
    units = gate_pre.shape[1]
    chunks = units // CHUNK
    ranks = 2 * RANK
    size = RANK * RANK // (mp_size * ranks)
    any_space = pl.BlockSpec(memory_space=pl.ANY)
    return pl.pallas_call(
        functools.partial(kernel, mp_size),
        out_shape=jax.ShapeDtypeStruct((1, ranks // mp_size, RANK), F32),
        in_specs=[any_space] * 7,
        out_specs=pl.BlockSpec(memory_space=pltpu.VMEM),
        scratch_shapes=[
            pltpu.VMEM((length, width), BF16),
            pltpu.VMEM((chunks, length, CHUNK), BF16),
            pltpu.VMEM((chunks, length, CHUNK), BF16),
            pltpu.VMEM((chunks, length, CHUNK), BF16),
            pltpu.VMEM((length, width), BF16),
            pltpu.VMEM((width, ranks), BF16),
            pltpu.VMEM((chunks, CHUNK, ranks), BF16),
            pltpu.VMEM((2, 2 * length, CHUNK), BF16),
            pltpu.VMEM((2, length, ranks), F32),
            pltpu.VMEM((length, ranks), F32),
            pltpu.VMEM((mp_size // NC, length, ranks), F32),
            pltpu.VMEM((ranks, ranks), F32),
            pltpu.VMEM((2, RANK, ranks), F32),
            pltpu.VMEM((mp_size, size, ranks), F32),
            pltpu.VMEM((NZ, size, ranks), F32),
            pltpu.VMEM((NY * mp_size, size, ranks), F32),
            pltpu.VMEM((RANK // 2, ranks), F32),
            pltpu.VMEM((ranks, ranks), F32),
            pltpu.SemaphoreType.DMA((3,)),
            pltpu.SemaphoreType.DMA((chunks, 4)),
            pltpu.SemaphoreType.DMA((2,)),
            pltpu.SemaphoreType.DMA((2,)),
            pltpu.SemaphoreType.DMA((2,)),
            pltpu.SemaphoreType.DMA((2,)),
            pltpu.SemaphoreType.DMA((2,)),
        ],
        compiler_params=pltpu.CompilerParams(collective_id=0, has_side_effects=True),
        name="whiten",
    )(tokens_in, gate_pre, up_pre, hidden_grad, out_grad, proj_model, proj_hidden)


def solution(mesh):
    in_specs = (
        P("dp", "mp"),
        P("dp", "mp"),
        P("dp", "mp"),
        P("dp", "mp"),
        P("dp", "mp"),
        P("mp", None),
        P("mp", None),
    )
    out_specs = P("dp", "mp", None)
    return jax.shard_map(shards, mesh=mesh, in_specs=in_specs, out_specs=out_specs, check_vma=False)
```

```python
import functools
import math

import jax
import jax.numpy as jnp
from jax import lax
from jax.experimental import pallas as pl
from jax.experimental.pallas import tpu as pltpu
from jax.sharding import PartitionSpec as P

RANK = 64
LEN = 128
NY, NZ = 4, 16
NC = 2
ROWS = 64
F32 = jnp.float32
BF16 = jnp.bfloat16
MESH = pl.DeviceIdType.MESH
NT = (((1,), (1,)), ((), ()))


def halves(value):
    high = value.astype(BF16)
    return high, (value - high.astype(F32)).astype(BF16)


def thirds(value):
    high = value.astype(BF16)
    rest = value - high.astype(F32)
    mid = rest.astype(BF16)
    return high, mid, (rest - mid.astype(F32)).astype(BF16)


def product_3(left, right):
    lh, ll = halves(left)
    rh, rl = halves(right)
    return lax.dot_general(
        jnp.concatenate([lh, lh, ll], axis=1),
        jnp.concatenate([rh, rl, rh], axis=1),
        NT,
        preferred_element_type=F32,
    )


def product_6(left, right):
    lh, lm, ll = thirds(left)
    rh, rm, rl = thirds(right)
    return lax.dot_general(
        jnp.concatenate([ll, lm, lh, lm, lh, lh], axis=1),
        jnp.concatenate([rh, rm, rl, rh, rm, rh], axis=1),
        NT,
        preferred_element_type=F32,
    )


def eliminate(table, rows_out):
    width = table.shape[1]
    tiles = [table[i : i + 8] for i in range(0, RANK, 8)]
    for t in range(RANK // 8):
        columns = [
            [jnp.broadcast_to(tile[:, 8 * t + j : 8 * t + j + 1], tile.shape) for tile in tiles[t:]] for j in range(8)
        ]
        rows = [jnp.broadcast_to(tiles[t][j : j + 1], (8, width)) for j in range(8)]
        pivot = [[jnp.broadcast_to(columns[j][0][i : i + 1], (8, width)) for j in range(i + 1)] for i in range(8)]
        scaled = []
        for j in range(8):
            inverse = 1.0 / pivot[j][j]
            rows_out[8 * t + j : 8 * t + j + 1, :] = (rows[j] * lax.rsqrt(pivot[j][j]))[:1]
            for m in range(j + 1, 8):
                share = pivot[m][j] * inverse
                rows[m] = rows[m] - share * rows[j]
                for n in range(j + 1, m + 1):
                    pivot[m][n] = pivot[m][n] - share * pivot[n][j]
                columns[m] = [late - share * early for late, early in zip(columns[m], columns[j])]
            scaled.append(rows[j] * inverse)
        for i in range(t + 1, RANK // 8):
            for j in range(8):
                tiles[i] = tiles[i] - columns[j][i - t] * scaled[j]


def kernel(
    mp_size,
    tokens_hbm,
    gate_hbm,
    up_hbm,
    hidden_grad_hbm,
    out_grad_hbm,
    model_hbm,
    hidden_hbm,
    out_ref,
    tokens,
    gate,
    up,
    hidden_grad,
    out_grad,
    model,
    hidden,
    lhs,
    part,
    from_core,
    xbuf,
    sbuf,
    mbuf,
    packed,
    zbuf,
    fbuf,
    aug,
    rows_out,
    in_sem,
    block_sem,
    core_sem,
    x_sem,
    m_sem,
    z_sem,
    f_sem,
):
    nx = mp_size // NC
    dp = lax.axis_index("dp")
    mp = lax.axis_index("mp")
    y, z = dp // NZ, dp % NZ
    x, core = mp // NC, mp % NC

    weights = pltpu.make_async_copy(hidden_hbm, hidden, in_sem.at[0])
    last = [
        pltpu.make_async_copy(model_hbm, model, in_sem.at[1]),
        pltpu.make_async_copy(tokens_hbm, tokens, in_sem.at[2]),
        pltpu.make_async_copy(out_grad_hbm, out_grad, in_sem.at[3]),
    ]
    weights.start()
    blocks = []
    for i in range(LEN // ROWS):
        span = pl.ds(i * ROWS, ROWS)
        group = [
            pltpu.make_async_copy(gate_hbm.at[span, :], gate.at[span, :], block_sem.at[i, 0]),
            pltpu.make_async_copy(hidden_grad_hbm.at[span, :], hidden_grad.at[span, :], block_sem.at[i, 1]),
            pltpu.make_async_copy(up_hbm.at[span, :], up.at[span, :], block_sem.at[i, 2]),
        ]
        for copy in group:
            copy.start()
        blocks.append(group)
    for copy in last:
        copy.start()

    barrier = pltpu.get_barrier_semaphore()
    plane = NY * mp_size

    def z_peer(apart):
        return (y * NZ + (z + apart) % NZ, mp)

    def plane_peer(apart):
        there = (y * mp_size + mp + apart) % plane
        return ((there // mp_size) * NZ + z, there % mp_size)

    def greet_z(apart, carry):
        pl.semaphore_signal(barrier, inc=1, device_id=z_peer(apart), device_id_type=MESH)
        return carry

    def greet_plane(apart, carry):
        pl.semaphore_signal(barrier, inc=1, device_id=plane_peer(apart), device_id_type=MESH)
        return carry

    lax.fori_loop(1, NZ, greet_z, 0)
    lax.fori_loop(1, plane, greet_plane, 0)

    weights.wait()
    upward, downward = [], []
    for i, group in enumerate(blocks):
        for copy in group:
            copy.wait()
        for r in range(i * ROWS, (i + 1) * ROWS, 32):
            span = pl.ds(r, 32)
            half = 0.5 * gate[span, :].astype(F32)
            act = half + half * jnp.tanh(half)
            lhs[0, span, :] = (hidden_grad[span, :].astype(F32) * act).astype(BF16)
            lhs[1, span, :] = (act * up[span, :].astype(F32)).astype(BF16)
        span = pl.ds(i * ROWS, ROWS)
        upward.append(jnp.dot(lhs[0, span, :], hidden[...], preferred_element_type=F32))
        downward.append(jnp.dot(lhs[1, span, :], hidden[...], preferred_element_type=F32))
    for copy in last:
        copy.wait()
    inward = jnp.dot(tokens[...], model[...], preferred_element_type=F32)
    outward = jnp.dot(out_grad[...], model[...], preferred_element_type=F32)
    lane = lax.broadcasted_iota(jnp.int32, (LEN, 2 * RANK), 1)
    low = lane < RANK
    part[0] = jnp.where(low, inward, pltpu.roll(jnp.concatenate(upward, axis=0), RANK, 1))
    part[1] = jnp.where(low, pltpu.roll(outward, RANK, 1), jnp.concatenate(downward, axis=0))

    pl.semaphore_wait(barrier, NZ - 1 + plane - 1)

    sibling = (dp, x * NC + 1 - core)
    swap = pltpu.make_async_remote_copy(
        part.at[1 - core], from_core, core_sem.at[0], core_sem.at[1], device_id=sibling, device_id_type=MESH
    )
    swap.start()
    swap.wait()
    xbuf[x] = part[core] + from_core[...]

    for apart in range(1, nx):
        pltpu.make_async_remote_copy(
            xbuf.at[x],
            xbuf.at[x],
            x_sem.at[0],
            x_sem.at[1],
            device_id=(dp, ((x + apart) % nx) * NC + core),
            device_id_type=MESH,
        ).start()
    all_x = pltpu.make_async_remote_copy(
        xbuf.at[pl.ds(0, nx - 1)],
        xbuf.at[pl.ds(0, nx - 1)],
        x_sem.at[0],
        x_sem.at[1],
        device_id=sibling,
        device_id_type=MESH,
    )
    all_x.wait_send()
    all_x.wait_recv()
    summed = xbuf[0]
    for i in range(1, nx):
        summed = summed + xbuf[i]

    turned = summed.T
    sbuf[...] = product_3(turned, turned)
    mine = pl.ds(pl.multiple_of((1 - core) * RANK, RANK), RANK)
    mbuf[core] = sbuf[mine, :]
    give = pltpu.make_async_remote_copy(
        mbuf.at[core], mbuf.at[core], m_sem.at[0], m_sem.at[1], device_id=sibling, device_id_type=MESH
    )
    give.start()
    give.wait()
    short_low = lax.broadcasted_iota(jnp.int32, (RANK, 2 * RANK), 1) < RANK
    stacked = jnp.where(short_low, mbuf[0], mbuf[1])

    gram = product_6(stacked, jnp.concatenate([stacked, stacked], axis=0))
    half_low = lax.broadcasted_iota(jnp.int32, (RANK // 2, 2 * RANK), 1) < RANK
    pairs = jnp.where(half_low, gram[: RANK // 2], gram[RANK // 2 :])
    size = packed.shape[1]
    for i in range(mp_size):
        packed[i] = pairs[i * size : (i + 1) * size]

    for apart in sorted(range(1, NZ), key=lambda d: -min(d, NZ - d)):
        pltpu.make_async_remote_copy(
            packed.at[mp], zbuf.at[z], z_sem.at[0], z_sem.at[1], device_id=z_peer(apart), device_id_type=MESH
        ).start()
    zbuf[z] = packed[mp]
    own = pltpu.roll(stacked, (RANK + 2 * RANK - mp * (2 * RANK // mp_size)) % (2 * RANK), 1)
    all_z = pltpu.make_async_remote_copy(
        zbuf.at[pl.ds(0, NZ - 1)],
        zbuf.at[pl.ds(0, NZ - 1)],
        z_sem.at[0],
        z_sem.at[1],
        device_id=sibling,
        device_id_type=MESH,
    )
    all_z.wait_send()
    all_z.wait_recv()
    slice_sum = zbuf[0]
    for i in range(1, NZ):
        slice_sum = slice_sum + zbuf[i]
    place = y * mp_size + mp
    fbuf[place] = slice_sum

    def send_plane(apart, carry):
        pltpu.make_async_remote_copy(
            fbuf.at[place], fbuf.at[place], f_sem.at[0], f_sem.at[1], device_id=plane_peer(apart), device_id_type=MESH
        ).start()
        return carry

    lax.fori_loop(1, plane, send_plane, 0)
    all_plane = pltpu.make_async_remote_copy(
        fbuf.at[pl.ds(0, plane - 1)],
        fbuf.at[pl.ds(0, plane - 1)],
        f_sem.at[0],
        f_sem.at[1],
        device_id=sibling,
        device_id_type=MESH,
    )
    all_plane.wait_send()
    all_plane.wait_recv()
    for i in range(mp_size):
        piece = fbuf[i]
        for j in range(1, NY):
            piece = piece + fbuf[j * mp_size + i]
        aug[i * size : (i + 1) * size, :] = piece
    folded = aug[...]
    whole = jnp.concatenate([folded, pltpu.roll(folded, RANK, 1)], axis=0)
    table = jnp.where(short_low, whole, own)

    eliminate(table, rows_out)
    factor = math.sqrt(NY * NZ * LEN)
    turned_out = rows_out[...].T
    out_ref[0] = turned_out[RANK : RANK + 2 * RANK // mp_size, :RANK] * factor


def shards(tokens_in, gate_pre, up_pre, hidden_grad, out_grad, proj_model, proj_hidden):
    mp_size = lax.axis_size("mp")
    length, width = tokens_in.shape
    units = gate_pre.shape[1]
    ranks = 2 * RANK
    size = RANK * RANK // (mp_size * ranks)
    any_space = pl.BlockSpec(memory_space=pl.ANY)
    return pl.pallas_call(
        functools.partial(kernel, mp_size),
        out_shape=pltpu.VMEM((1, ranks // mp_size, RANK), F32),
        in_specs=[any_space] * 7,
        out_specs=pl.BlockSpec(memory_space=pltpu.VMEM),
        scratch_shapes=[
            pltpu.VMEM((length, width), BF16),
            pltpu.VMEM((length, units), BF16),
            pltpu.VMEM((length, units), BF16),
            pltpu.VMEM((length, units), BF16),
            pltpu.VMEM((length, width), BF16),
            pltpu.VMEM((width, ranks), BF16),
            pltpu.VMEM((units, ranks), BF16),
            pltpu.VMEM((2, length, units), BF16),
            pltpu.VMEM((2, length, ranks), F32),
            pltpu.VMEM((length, ranks), F32),
            pltpu.VMEM((mp_size // NC, length, ranks), F32),
            pltpu.VMEM((ranks, ranks), F32),
            pltpu.VMEM((2, RANK, ranks), F32),
            pltpu.VMEM((mp_size, size, ranks), F32),
            pltpu.VMEM((NZ, size, ranks), F32),
            pltpu.VMEM((NY * mp_size, size, ranks), F32),
            pltpu.VMEM((RANK // 2, ranks), F32),
            pltpu.VMEM((ranks, ranks), F32),
            pltpu.SemaphoreType.DMA((4,)),
            pltpu.SemaphoreType.DMA((LEN // ROWS, 3)),
            pltpu.SemaphoreType.DMA((2,)),
            pltpu.SemaphoreType.DMA((2,)),
            pltpu.SemaphoreType.DMA((2,)),
            pltpu.SemaphoreType.DMA((2,)),
            pltpu.SemaphoreType.DMA((2,)),
        ],
        compiler_params=pltpu.CompilerParams(collective_id=0, has_side_effects=True),
        name="whiten",
    )(tokens_in, gate_pre, up_pre, hidden_grad, out_grad, proj_model, proj_hidden)


def solution(mesh):
    in_specs = (
        P("dp", "mp"),
        P("dp", "mp"),
        P("dp", "mp"),
        P("dp", "mp"),
        P("dp", "mp"),
        P("mp", None),
        P("mp", None),
    )
    out_specs = P("dp", "mp", None)
    return jax.shard_map(shards, mesh=mesh, in_specs=in_specs, out_specs=out_specs, check_vma=False)
```

```python
import functools
import math

import jax
import jax.numpy as jnp
from jax import lax
from jax.experimental import pallas as pl
from jax.experimental.pallas import tpu as pltpu
from jax.sharding import PartitionSpec as P

RANK = 64
LEN = 128
NY, NZ = 4, 16
NC = 2
ROWS = 64
F32 = jnp.float32
BF16 = jnp.bfloat16
MESH = pl.DeviceIdType.MESH
NT = (((1,), (1,)), ((), ()))


def halves(value):
    high = value.astype(BF16)
    return high, (value - high.astype(F32)).astype(BF16)


def thirds(value):
    high = value.astype(BF16)
    rest = value - high.astype(F32)
    mid = rest.astype(BF16)
    return high, mid, (rest - mid.astype(F32)).astype(BF16)


def product_3(left, right):
    lh, ll = halves(left)
    rh, rl = halves(right)
    return lax.dot_general(
        jnp.concatenate([lh, lh, ll], axis=1),
        jnp.concatenate([rh, rl, rh], axis=1),
        NT,
        preferred_element_type=F32,
    )


def product_6(left, right):
    lh, lm, ll = thirds(left)
    rh, rm, rl = thirds(right)
    return lax.dot_general(
        jnp.concatenate([ll, lm, lh, lm, lh, lh], axis=1),
        jnp.concatenate([rh, rm, rl, rh, rm, rh], axis=1),
        NT,
        preferred_element_type=F32,
    )


def eliminate(table, rows_out):
    width = table.shape[1]
    tiles = [table[i : i + 8] for i in range(0, RANK, 8)]
    for t in range(RANK // 8):
        columns = [
            [jnp.broadcast_to(tile[:, 8 * t + j : 8 * t + j + 1], tile.shape) for tile in tiles[t:]] for j in range(8)
        ]
        rows = [jnp.broadcast_to(tiles[t][j : j + 1], (8, width)) for j in range(8)]
        pivot = [[jnp.broadcast_to(columns[j][0][i : i + 1], (8, width)) for j in range(i + 1)] for i in range(8)]
        scaled = []
        for j in range(8):
            inverse = 1.0 / pivot[j][j]
            rows_out[8 * t + j : 8 * t + j + 1, :] = (rows[j] * lax.rsqrt(pivot[j][j]))[:1]
            for m in range(j + 1, 8):
                share = pivot[m][j] * inverse
                rows[m] = rows[m] - share * rows[j]
                for n in range(j + 1, m + 1):
                    pivot[m][n] = pivot[m][n] - share * pivot[n][j]
                columns[m] = [late - share * early for late, early in zip(columns[m], columns[j])]
            scaled.append(rows[j] * inverse)
        for i in range(t + 1, RANK // 8):
            for j in range(8):
                tiles[i] = tiles[i] - columns[j][i - t] * scaled[j]


def kernel(
    mp_size,
    tokens_hbm,
    gate_hbm,
    up_hbm,
    hidden_grad_hbm,
    out_grad_hbm,
    model_hbm,
    hidden_hbm,
    out_ref,
    tokens,
    gate,
    up,
    hidden_grad,
    out_grad,
    model,
    hidden,
    lhs,
    part,
    from_core,
    xbuf,
    sbuf,
    mbuf,
    packed,
    zbuf,
    fbuf,
    aug,
    rows_out,
    in_sem,
    block_sem,
    core_sem,
    x_sem,
    m_sem,
    z_sem,
    f_sem,
    far_sem,
):
    nx = mp_size // NC
    dp = lax.axis_index("dp")
    mp = lax.axis_index("mp")
    y, z = dp // NZ, dp % NZ
    x, core = mp // NC, mp % NC

    weights = pltpu.make_async_copy(hidden_hbm, hidden, in_sem.at[0])
    last = [
        pltpu.make_async_copy(model_hbm, model, in_sem.at[1]),
        pltpu.make_async_copy(tokens_hbm, tokens, in_sem.at[2]),
        pltpu.make_async_copy(out_grad_hbm, out_grad, in_sem.at[3]),
    ]
    weights.start()
    blocks = []
    for i in range(LEN // ROWS):
        span = pl.ds(i * ROWS, ROWS)
        group = [
            pltpu.make_async_copy(gate_hbm.at[span, :], gate.at[span, :], block_sem.at[i, 0]),
            pltpu.make_async_copy(hidden_grad_hbm.at[span, :], hidden_grad.at[span, :], block_sem.at[i, 1]),
            pltpu.make_async_copy(up_hbm.at[span, :], up.at[span, :], block_sem.at[i, 2]),
        ]
        for copy in group:
            copy.start()
        blocks.append(group)
    for copy in last:
        copy.start()

    barrier = pltpu.get_barrier_semaphore()
    plane = NY * mp_size

    def z_peer(apart):
        return (y * NZ + (z + apart) % NZ, mp)

    def plane_peer(apart):
        there = (y * mp_size + mp + apart) % plane
        return ((there // mp_size) * NZ + z, there % mp_size)

    def along_z(semaphore, steps):
        for apart in steps:
            for way in (apart, NZ - apart):
                pl.semaphore_signal(semaphore, inc=1, device_id=z_peer(way), device_id_type=MESH)

    for apart in range(1, mp_size):
        pl.semaphore_signal(barrier, inc=1, device_id=(dp, (mp + apart) % mp_size), device_id_type=MESH)
    for apart in range(1, NY):
        there = ((y + apart) % NY) * NZ + z
        pl.semaphore_signal(barrier, inc=1, device_id=(there, mp), device_id_type=MESH)
    along_z(barrier, (1, 2))

    weights.wait()
    upward, downward = [], []
    for i, group in enumerate(blocks):
        for copy in group:
            copy.wait()
        for r in range(i * ROWS, (i + 1) * ROWS, 32):
            span = pl.ds(r, 32)
            half = 0.5 * gate[span, :].astype(F32)
            act = half + half * jnp.tanh(half)
            lhs[0, span, :] = (hidden_grad[span, :].astype(F32) * act).astype(BF16)
            lhs[1, span, :] = (act * up[span, :].astype(F32)).astype(BF16)
        span = pl.ds(i * ROWS, ROWS)
        upward.append(jnp.dot(lhs[0, span, :], hidden[...], preferred_element_type=F32))
        downward.append(jnp.dot(lhs[1, span, :], hidden[...], preferred_element_type=F32))
    for copy in last:
        copy.wait()
    inward = jnp.dot(tokens[...], model[...], preferred_element_type=F32)
    outward = jnp.dot(out_grad[...], model[...], preferred_element_type=F32)
    lane = lax.broadcasted_iota(jnp.int32, (LEN, 2 * RANK), 1)
    low = lane < RANK
    part[0] = jnp.where(low, inward, pltpu.roll(jnp.concatenate(upward, axis=0), RANK, 1))
    part[1] = jnp.where(low, pltpu.roll(outward, RANK, 1), jnp.concatenate(downward, axis=0))

    pl.semaphore_wait(barrier, mp_size - 1 + NY - 1 + 4)
    along_z(far_sem.at[0], (2,))

    sibling = (dp, x * NC + 1 - core)
    swap = pltpu.make_async_remote_copy(
        part.at[1 - core], from_core, core_sem.at[0], core_sem.at[1], device_id=sibling, device_id_type=MESH
    )
    swap.start()
    swap.wait_recv()
    xbuf[x] = part[core] + from_core[...]

    for apart in range(1, nx):
        pltpu.make_async_remote_copy(
            xbuf.at[x],
            xbuf.at[x],
            x_sem.at[0],
            x_sem.at[1],
            device_id=(dp, ((x + apart) % nx) * NC + core),
            device_id_type=MESH,
        ).start()
    pl.semaphore_wait(far_sem.at[0], 2)
    along_z(far_sem.at[1], (4,))
    all_x = pltpu.make_async_remote_copy(
        xbuf.at[pl.ds(0, nx - 1)],
        xbuf.at[pl.ds(0, nx - 1)],
        x_sem.at[0],
        x_sem.at[1],
        device_id=sibling,
        device_id_type=MESH,
    )
    all_x.wait_recv()
    summed = xbuf[0]
    for i in range(1, nx):
        summed = summed + xbuf[i]

    turned = summed.T
    sbuf[...] = product_3(turned, turned)
    mine = pl.ds(pl.multiple_of((1 - core) * RANK, RANK), RANK)
    mbuf[core] = sbuf[mine, :]
    give = pltpu.make_async_remote_copy(
        mbuf.at[core], mbuf.at[core], m_sem.at[0], m_sem.at[1], device_id=sibling, device_id_type=MESH
    )
    give.start()
    give.wait_recv()
    short_low = lax.broadcasted_iota(jnp.int32, (RANK, 2 * RANK), 1) < RANK
    stacked = jnp.where(short_low, mbuf[0], mbuf[1])

    gram = product_6(stacked, jnp.concatenate([stacked, stacked], axis=0))
    half_low = lax.broadcasted_iota(jnp.int32, (RANK // 2, 2 * RANK), 1) < RANK
    pairs = jnp.where(half_low, gram[: RANK // 2], gram[RANK // 2 :])
    size = packed.shape[1]
    for i in range(mp_size):
        packed[i] = pairs[i * size : (i + 1) * size]

    pl.semaphore_wait(far_sem.at[1], 2)
    for apart in sorted(range(1, NZ), key=lambda d: -min(d, NZ - d)):
        pltpu.make_async_remote_copy(
            packed.at[mp], zbuf.at[z], z_sem.at[0], z_sem.at[1], device_id=z_peer(apart), device_id_type=MESH
        ).start()
    zbuf[z] = packed[mp]
    own = pltpu.roll(stacked, (RANK + 2 * RANK - mp * (2 * RANK // mp_size)) % (2 * RANK), 1)
    all_z = pltpu.make_async_remote_copy(
        zbuf.at[pl.ds(0, NZ - 1)],
        zbuf.at[pl.ds(0, NZ - 1)],
        z_sem.at[0],
        z_sem.at[1],
        device_id=sibling,
        device_id_type=MESH,
    )
    all_z.wait_recv()
    slice_sum = zbuf[0]
    for i in range(1, NZ):
        slice_sum = slice_sum + zbuf[i]
    place = y * mp_size + mp
    fbuf[place] = slice_sum

    def send_plane(apart, carry):
        pltpu.make_async_remote_copy(
            fbuf.at[place], fbuf.at[place], f_sem.at[0], f_sem.at[1], device_id=plane_peer(apart), device_id_type=MESH
        ).start()
        return carry

    lax.fori_loop(1, plane, send_plane, 0)
    all_plane = pltpu.make_async_remote_copy(
        fbuf.at[pl.ds(0, plane - 1)],
        fbuf.at[pl.ds(0, plane - 1)],
        f_sem.at[0],
        f_sem.at[1],
        device_id=sibling,
        device_id_type=MESH,
    )
    all_plane.wait_recv()
    for i in range(mp_size):
        piece = fbuf[i]
        for j in range(1, NY):
            piece = piece + fbuf[j * mp_size + i]
        aug[i * size : (i + 1) * size, :] = piece
    folded = aug[...]
    whole = jnp.concatenate([folded, pltpu.roll(folded, RANK, 1)], axis=0)
    table = jnp.where(short_low, whole, own)

    eliminate(table, rows_out)
    factor = math.sqrt(NY * NZ * LEN)
    turned_out = rows_out[...].T
    out_ref[0] = turned_out[RANK : RANK + 2 * RANK // mp_size, :RANK] * factor

    for sent in (swap, all_x, give, all_z, all_plane):
        sent.wait_send()

def shards(tokens_in, gate_pre, up_pre, hidden_grad, out_grad, proj_model, proj_hidden):
    mp_size = lax.axis_size("mp")
    length, width = tokens_in.shape
    units = gate_pre.shape[1]
    ranks = 2 * RANK
    size = RANK * RANK // (mp_size * ranks)
    any_space = pl.BlockSpec(memory_space=pl.ANY)
    return pl.pallas_call(
        functools.partial(kernel, mp_size),
        out_shape=pltpu.VMEM((1, ranks // mp_size, RANK), F32),
        in_specs=[any_space] * 7,
        out_specs=pl.BlockSpec(memory_space=pltpu.VMEM),
        scratch_shapes=[
            pltpu.VMEM((length, width), BF16),
            pltpu.VMEM((length, units), BF16),
            pltpu.VMEM((length, units), BF16),
            pltpu.VMEM((length, units), BF16),
            pltpu.VMEM((length, width), BF16),
            pltpu.VMEM((width, ranks), BF16),
            pltpu.VMEM((units, ranks), BF16),
            pltpu.VMEM((2, length, units), BF16),
            pltpu.VMEM((2, length, ranks), F32),
            pltpu.VMEM((length, ranks), F32),
            pltpu.VMEM((mp_size // NC, length, ranks), F32),
            pltpu.VMEM((ranks, ranks), F32),
            pltpu.VMEM((2, RANK, ranks), F32),
            pltpu.VMEM((mp_size, size, ranks), F32),
            pltpu.VMEM((NZ, size, ranks), F32),
            pltpu.VMEM((NY * mp_size, size, ranks), F32),
            pltpu.VMEM((RANK // 2, ranks), F32),
            pltpu.VMEM((ranks, ranks), F32),
            pltpu.SemaphoreType.DMA((4,)),
            pltpu.SemaphoreType.DMA((LEN // ROWS, 3)),
            pltpu.SemaphoreType.DMA((2,)),
            pltpu.SemaphoreType.DMA((2,)),
            pltpu.SemaphoreType.DMA((2,)),
            pltpu.SemaphoreType.DMA((2,)),
            pltpu.SemaphoreType.DMA((2,)),
            pltpu.SemaphoreType.REGULAR((2,)),
        ],
        compiler_params=pltpu.CompilerParams(collective_id=0, has_side_effects=True),
        name="whiten",
    )(tokens_in, gate_pre, up_pre, hidden_grad, out_grad, proj_model, proj_hidden)


def solution(mesh):
    in_specs = (
        P("dp", "mp"),
        P("dp", "mp"),
        P("dp", "mp"),
        P("dp", "mp"),
        P("dp", "mp"),
        P("mp", None),
        P("mp", None),
    )
    out_specs = P("dp", "mp", None)
    return jax.shard_map(shards, mesh=mesh, in_specs=in_specs, out_specs=out_specs, check_vma=False)
```

```python
import functools
import math

import jax
import jax.numpy as jnp
from jax import lax
from jax.experimental import pallas as pl
from jax.experimental.pallas import tpu as pltpu
from jax.sharding import PartitionSpec as P

RANK = 64
LEN = 128
NY, NZ = 4, 16
NC = 2
ROWS = 64
F32 = jnp.float32
BF16 = jnp.bfloat16
MESH = pl.DeviceIdType.MESH
NT = (((1,), (1,)), ((), ()))


def hops(apart, size):
    return min(apart, size - apart)


def farthest_first(size):
    return sorted(range(1, size), key=lambda apart: -hops(apart, size))


def halves(value):
    high = value.astype(BF16)
    return high, (value - high.astype(F32)).astype(BF16)


def thirds(value):
    high = value.astype(BF16)
    rest = value - high.astype(F32)
    mid = rest.astype(BF16)
    return high, mid, (rest - mid.astype(F32)).astype(BF16)


def product_3(left, right):
    lh, ll = halves(left)
    rh, rl = halves(right)
    return lax.dot_general(
        jnp.concatenate([lh, lh, ll], axis=1),
        jnp.concatenate([rh, rl, rh], axis=1),
        NT,
        preferred_element_type=F32,
    )


def product_6(left, right):
    lh, lm, ll = thirds(left)
    rh, rm, rl = thirds(right)
    return lax.dot_general(
        jnp.concatenate([ll, lm, lh, lm, lh, lh], axis=1),
        jnp.concatenate([rh, rm, rl, rh, rm, rh], axis=1),
        NT,
        preferred_element_type=F32,
    )


def eliminate(table, rows_out):
    width = table.shape[1]
    tiles = [table[i : i + 8] for i in range(0, RANK, 8)]
    for t in range(RANK // 8):
        columns = [
            [jnp.broadcast_to(tile[:, 8 * t + j : 8 * t + j + 1], tile.shape) for tile in tiles[t:]] for j in range(8)
        ]
        rows = [jnp.broadcast_to(tiles[t][j : j + 1], (8, width)) for j in range(8)]
        pivot = [[jnp.broadcast_to(columns[j][0][i : i + 1], (8, width)) for j in range(i + 1)] for i in range(8)]
        scaled = []
        for j in range(8):
            inverse = 1.0 / pivot[j][j]
            rows_out[8 * t + j : 8 * t + j + 1, :] = (rows[j] * lax.rsqrt(pivot[j][j]))[:1]
            for m in range(j + 1, 8):
                share = pivot[m][j] * inverse
                rows[m] = rows[m] - share * rows[j]
                for n in range(j + 1, m + 1):
                    pivot[m][n] = pivot[m][n] - share * pivot[n][j]
                columns[m] = [late - share * early for late, early in zip(columns[m], columns[j])]
            scaled.append(rows[j] * inverse)
        for i in range(t + 1, RANK // 8):
            for j in range(8):
                tiles[i] = tiles[i] - columns[j][i - t] * scaled[j]


def kernel(
    mp_size,
    tokens_hbm,
    gate_hbm,
    up_hbm,
    hidden_grad_hbm,
    out_grad_hbm,
    model_hbm,
    hidden_hbm,
    out_ref,
    tokens,
    gate,
    up,
    hidden_grad,
    out_grad,
    model,
    hidden,
    lhs,
    part,
    from_core,
    xbuf,
    sbuf,
    mbuf,
    packed,
    zbuf,
    fbuf,
    aug,
    rows_out,
    in_sem,
    block_sem,
    core_sem,
    x_sem,
    m_sem,
    z_sem,
    f_sem,
    far_sem,
):
    nx = mp_size // NC
    dp = lax.axis_index("dp")
    mp = lax.axis_index("mp")
    y, z = dp // NZ, dp % NZ
    x, core = mp // NC, mp % NC

    weights = pltpu.make_async_copy(hidden_hbm, hidden, in_sem.at[0])
    last = [
        pltpu.make_async_copy(model_hbm, model, in_sem.at[1]),
        pltpu.make_async_copy(tokens_hbm, tokens, in_sem.at[2]),
        pltpu.make_async_copy(out_grad_hbm, out_grad, in_sem.at[3]),
    ]
    weights.start()
    blocks = []
    for i in range(LEN // ROWS):
        span = pl.ds(i * ROWS, ROWS)
        group = [
            pltpu.make_async_copy(gate_hbm.at[span, :], gate.at[span, :], block_sem.at[i, 0]),
            pltpu.make_async_copy(hidden_grad_hbm.at[span, :], hidden_grad.at[span, :], block_sem.at[i, 1]),
            pltpu.make_async_copy(up_hbm.at[span, :], up.at[span, :], block_sem.at[i, 2]),
        ]
        for copy in group:
            copy.start()
        blocks.append(group)
    for copy in last:
        copy.start()

    barrier = pltpu.get_barrier_semaphore()
    plane = NY * mp_size

    def z_peer(apart, other):
        return (y * NZ + (z + apart) % NZ, x * NC + (core + other) % NC)

    def plane_peer(far_y, far_x, other):
        return ((y + far_y) % NY) * NZ + z, ((x + far_x) % nx) * NC + (core + other) % NC

    def along_z(semaphore, steps, cores):
        for apart in steps:
            for way in (apart, NZ - apart):
                for other in range(cores):
                    pl.semaphore_signal(semaphore, inc=1, device_id=z_peer(way, other), device_id_type=MESH)

    for apart in range(1, mp_size):
        pl.semaphore_signal(barrier, inc=1, device_id=(dp, (mp + apart) % mp_size), device_id_type=MESH)
    for apart in range(1, NY):
        there = ((y + apart) % NY) * NZ + z
        pl.semaphore_signal(barrier, inc=1, device_id=(there, mp), device_id_type=MESH)
    along_z(barrier, (1, 2), NC)

    weights.wait()
    upward, downward = [], []
    for i, group in enumerate(blocks):
        for copy in group:
            copy.wait()
        for r in range(i * ROWS, (i + 1) * ROWS, 32):
            span = pl.ds(r, 32)
            half = 0.5 * gate[span, :].astype(F32)
            act = half + half * jnp.tanh(half)
            lhs[0, span, :] = (hidden_grad[span, :].astype(F32) * act).astype(BF16)
            lhs[1, span, :] = (act * up[span, :].astype(F32)).astype(BF16)
        span = pl.ds(i * ROWS, ROWS)
        upward.append(jnp.dot(lhs[0, span, :], hidden[...], preferred_element_type=F32))
        downward.append(jnp.dot(lhs[1, span, :], hidden[...], preferred_element_type=F32))
    for copy in last:
        copy.wait()
    inward = jnp.dot(tokens[...], model[...], preferred_element_type=F32)
    outward = jnp.dot(out_grad[...], model[...], preferred_element_type=F32)
    lane = lax.broadcasted_iota(jnp.int32, (LEN, 2 * RANK), 1)
    low = lane < RANK
    part[0] = jnp.where(low, inward, pltpu.roll(jnp.concatenate(upward, axis=0), RANK, 1))
    part[1] = jnp.where(low, pltpu.roll(outward, RANK, 1), jnp.concatenate(downward, axis=0))

    pl.semaphore_wait(barrier, mp_size - 1 + NY - 1 + 4 * NC)
    along_z(far_sem.at[0], (2,), 1)

    sibling = (dp, x * NC + 1 - core)
    swap = pltpu.make_async_remote_copy(
        part.at[1 - core], from_core, core_sem.at[0], core_sem.at[1], device_id=sibling, device_id_type=MESH
    )
    swap.start()
    swap.wait_recv()
    xbuf[x] = part[core] + from_core[...]

    for apart in farthest_first(nx):
        pltpu.make_async_remote_copy(
            xbuf.at[x],
            xbuf.at[x],
            x_sem.at[0],
            x_sem.at[1],
            device_id=(dp, ((x + apart) % nx) * NC + core),
            device_id_type=MESH,
        ).start()
    pl.semaphore_wait(far_sem.at[0], 2)
    along_z(far_sem.at[1], (4,), 1)
    all_x = pltpu.make_async_remote_copy(
        xbuf.at[pl.ds(0, nx - 1)],
        xbuf.at[pl.ds(0, nx - 1)],
        x_sem.at[0],
        x_sem.at[1],
        device_id=sibling,
        device_id_type=MESH,
    )
    all_x.wait_recv()
    summed = xbuf[0]
    for i in range(1, nx):
        summed = summed + xbuf[i]

    turned = summed.T
    sbuf[...] = product_3(turned, turned)
    mine = pl.ds(pl.multiple_of((1 - core) * RANK, RANK), RANK)
    mbuf[core] = sbuf[mine, :]
    give = pltpu.make_async_remote_copy(
        mbuf.at[core], mbuf.at[core], m_sem.at[0], m_sem.at[1], device_id=sibling, device_id_type=MESH
    )
    give.start()

    short_lane = lax.broadcasted_iota(jnp.int32, (RANK, 2 * RANK), 1)
    block = jnp.where(short_lane // RANK == core, mbuf[core], 0.0)
    gram = product_6(block, jnp.concatenate([block, block], axis=0))
    half_low = lax.broadcasted_iota(jnp.int32, (RANK // 2, 2 * RANK), 1) < RANK
    pairs = jnp.where(half_low, gram[: RANK // 2], gram[RANK // 2 :])
    size = packed.shape[1]
    for i in range(mp_size):
        packed[i] = pairs[i * size : (i + 1) * size]

    pl.semaphore_wait(far_sem.at[1], 2)
    slot = z * NC + core
    for apart in farthest_first(NZ):
        for other in range(NC):
            pltpu.make_async_remote_copy(
                packed.at[x * NC + (core + other) % NC],
                zbuf.at[slot],
                z_sem.at[0],
                z_sem.at[1],
                device_id=z_peer(apart, other),
                device_id_type=MESH,
            ).start()
    pltpu.make_async_remote_copy(
        packed.at[x * NC + 1 - core],
        zbuf.at[slot],
        z_sem.at[0],
        z_sem.at[1],
        device_id=sibling,
        device_id_type=MESH,
    ).start()
    zbuf[slot] = packed[mp]
    give.wait_recv()
    stacked = jnp.where(short_lane < RANK, mbuf[0], mbuf[1])
    own = pltpu.roll(stacked, (RANK + 2 * RANK - mp * (2 * RANK // mp_size)) % (2 * RANK), 1)
    all_z = pltpu.make_async_remote_copy(
        zbuf.at[pl.ds(0, NC * NZ - 1)],
        zbuf.at[pl.ds(0, NC * NZ - 1)],
        z_sem.at[0],
        z_sem.at[1],
        device_id=sibling,
        device_id_type=MESH,
    )
    all_z.wait_recv()
    terms = [zbuf[i] for i in range(NC * NZ)]
    while len(terms) > 1:
        terms = [first + second for first, second in zip(terms[::2], terms[1::2])]
    slice_sum = terms[0]
    place = y * mp_size + mp
    fbuf[place] = slice_sum

    others = [(i, j, k) for i in range(NY) for j in range(nx) for k in range(NC)][1:]
    for far in sorted(others, key=lambda far: -hops(far[0], NY) - hops(far[1], nx)):
        pltpu.make_async_remote_copy(
            fbuf.at[place], fbuf.at[place], f_sem.at[0], f_sem.at[1], device_id=plane_peer(*far), device_id_type=MESH
        ).start()
    all_plane = pltpu.make_async_remote_copy(
        fbuf.at[pl.ds(0, plane - 1)],
        fbuf.at[pl.ds(0, plane - 1)],
        f_sem.at[0],
        f_sem.at[1],
        device_id=sibling,
        device_id_type=MESH,
    )
    all_plane.wait_recv()
    for i in range(mp_size):
        piece = fbuf[i]
        for j in range(1, NY):
            piece = piece + fbuf[j * mp_size + i]
        aug[i * size : (i + 1) * size, :] = piece
    folded = aug[...]
    whole = jnp.concatenate([folded, pltpu.roll(folded, RANK, 1)], axis=0)
    table = jnp.where(short_lane < RANK, whole, own)

    eliminate(table, rows_out)
    factor = math.sqrt(NY * NZ * LEN)
    turned_out = rows_out[...].T
    out_ref[0] = turned_out[RANK : RANK + 2 * RANK // mp_size, :RANK] * factor

    for sent in (swap, all_x, give, all_z, all_plane):
        sent.wait_send()

def shards(tokens_in, gate_pre, up_pre, hidden_grad, out_grad, proj_model, proj_hidden):
    mp_size = lax.axis_size("mp")
    length, width = tokens_in.shape
    units = gate_pre.shape[1]
    ranks = 2 * RANK
    size = RANK * RANK // (mp_size * ranks)
    any_space = pl.BlockSpec(memory_space=pl.ANY)
    return pl.pallas_call(
        functools.partial(kernel, mp_size),
        out_shape=pltpu.VMEM((1, ranks // mp_size, RANK), F32),
        in_specs=[any_space] * 7,
        out_specs=pl.BlockSpec(memory_space=pltpu.VMEM),
        scratch_shapes=[
            pltpu.VMEM((length, width), BF16),
            pltpu.VMEM((length, units), BF16),
            pltpu.VMEM((length, units), BF16),
            pltpu.VMEM((length, units), BF16),
            pltpu.VMEM((length, width), BF16),
            pltpu.VMEM((width, ranks), BF16),
            pltpu.VMEM((units, ranks), BF16),
            pltpu.VMEM((2, length, units), BF16),
            pltpu.VMEM((2, length, ranks), F32),
            pltpu.VMEM((length, ranks), F32),
            pltpu.VMEM((mp_size // NC, length, ranks), F32),
            pltpu.VMEM((ranks, ranks), F32),
            pltpu.VMEM((2, RANK, ranks), F32),
            pltpu.VMEM((mp_size, size, ranks), F32),
            pltpu.VMEM((NC * NZ, size, ranks), F32),
            pltpu.VMEM((NY * mp_size, size, ranks), F32),
            pltpu.VMEM((RANK // 2, ranks), F32),
            pltpu.VMEM((ranks, ranks), F32),
            pltpu.SemaphoreType.DMA((4,)),
            pltpu.SemaphoreType.DMA((LEN // ROWS, 3)),
            pltpu.SemaphoreType.DMA((2,)),
            pltpu.SemaphoreType.DMA((2,)),
            pltpu.SemaphoreType.DMA((2,)),
            pltpu.SemaphoreType.DMA((2,)),
            pltpu.SemaphoreType.DMA((2,)),
            pltpu.SemaphoreType.REGULAR((2,)),
        ],
        compiler_params=pltpu.CompilerParams(collective_id=0, has_side_effects=True),
        name="whiten",
    )(tokens_in, gate_pre, up_pre, hidden_grad, out_grad, proj_model, proj_hidden)


def solution(mesh):
    in_specs = (
        P("dp", "mp"),
        P("dp", "mp"),
        P("dp", "mp"),
        P("dp", "mp"),
        P("dp", "mp"),
        P("mp", None),
        P("mp", None),
    )
    out_specs = P("dp", "mp", None)
    return jax.shard_map(shards, mesh=mesh, in_specs=in_specs, out_specs=out_specs, check_vma=False)
```

```python
import functools
import math

import jax
import jax.numpy as jnp
from jax import lax
from jax.experimental import pallas as pl
from jax.experimental.pallas import tpu as pltpu
from jax.sharding import PartitionSpec as P

RANK = 64
LEN = 128
NY, NZ = 4, 16
NC = 2
ROWS = 64
F32 = jnp.float32
BF16 = jnp.bfloat16
MESH = pl.DeviceIdType.MESH
NT = (((1,), (1,)), ((), ()))
TN = (((0,), (0,)), ((), ()))


def hops(apart, size):
    return min(apart, size - apart)


def farthest_first(size):
    return sorted(range(1, size), key=lambda apart: -hops(apart, size))


def halves(value):
    high = value.astype(BF16)
    return high, (value - high.astype(F32)).astype(BF16)


def thirds(value):
    high = value.astype(BF16)
    rest = value - high.astype(F32)
    mid = rest.astype(BF16)
    return high, mid, (rest - mid.astype(F32)).astype(BF16)


def product_3(left, right):
    lh, ll = halves(left)
    rh, rl = halves(right)
    return lax.dot_general(
        jnp.concatenate([lh, lh, ll], axis=0),
        jnp.concatenate([rh, rl, rh], axis=0),
        TN,
        preferred_element_type=F32,
    )


def product_6(left, right):
    lh, lm, ll = thirds(left)
    rh, rm, rl = thirds(right)
    return lax.dot_general(
        jnp.concatenate([ll, lm, lh, lm, lh, lh], axis=1),
        jnp.concatenate([rh, rm, rl, rh, rm, rh], axis=1),
        NT,
        preferred_element_type=F32,
    )


def eliminate(table, rows_out):
    width = table.shape[1]
    tiles = [table[i : i + 8] for i in range(0, RANK, 8)]
    for t in range(RANK // 8):
        columns = [
            [jnp.broadcast_to(tile[:, 8 * t + j : 8 * t + j + 1], tile.shape) for tile in tiles[t:]] for j in range(8)
        ]
        rows = [jnp.broadcast_to(tiles[t][j : j + 1], (8, width)) for j in range(8)]
        pivot = [[jnp.broadcast_to(columns[j][0][i : i + 1], (8, width)) for j in range(i + 1)] for i in range(8)]
        scaled = []
        for j in range(8):
            inverse = 1.0 / pivot[j][j]
            rows_out[8 * t + j : 8 * t + j + 1, :] = (rows[j] * lax.rsqrt(pivot[j][j]))[:1]
            for m in range(j + 1, 8):
                share = pivot[m][j] * inverse
                rows[m] = rows[m] - share * rows[j]
                for n in range(j + 1, m + 1):
                    pivot[m][n] = pivot[m][n] - share * pivot[n][j]
                columns[m] = [late - share * early for late, early in zip(columns[m], columns[j])]
            scaled.append(rows[j] * inverse)
        for i in range(t + 1, RANK // 8):
            for j in range(8):
                tiles[i] = tiles[i] - columns[j][i - t] * scaled[j]


def kernel(
    mp_size,
    tokens_hbm,
    gate_hbm,
    up_hbm,
    hidden_grad_hbm,
    out_grad_hbm,
    model_hbm,
    hidden_hbm,
    out_ref,
    tokens,
    gate,
    up,
    hidden_grad,
    out_grad,
    model,
    hidden,
    lhs,
    part,
    from_core,
    xbuf,
    mbuf,
    packed,
    zbuf,
    fbuf,
    aug,
    rows_out,
    in_sem,
    block_sem,
    core_sem,
    x_sem,
    m_sem,
    z_sem,
    f_sem,
    far_sem,
):
    nx = mp_size // NC
    dp = lax.axis_index("dp")
    mp = lax.axis_index("mp")
    y, z = dp // NZ, dp % NZ
    x, core = mp // NC, mp % NC

    weights = pltpu.make_async_copy(hidden_hbm, hidden, in_sem.at[0])
    side = [
        pltpu.make_async_copy(model_hbm, model, in_sem.at[1]),
        pltpu.make_async_copy(tokens_hbm, tokens, in_sem.at[2]),
        pltpu.make_async_copy(out_grad_hbm, out_grad, in_sem.at[3]),
    ]
    weights.start()
    blocks = []
    for i in range(LEN // ROWS):
        span = pl.ds(i * ROWS, ROWS)
        group = [
            pltpu.make_async_copy(gate_hbm.at[span, :], gate.at[span, :], block_sem.at[i, 0]),
            pltpu.make_async_copy(hidden_grad_hbm.at[span, :], hidden_grad.at[span, :], block_sem.at[i, 1]),
            pltpu.make_async_copy(up_hbm.at[span, :], up.at[span, :], block_sem.at[i, 2]),
        ]
        blocks.append(group)
    for copy in blocks[0] + side + blocks[1]:
        copy.start()

    barrier = pltpu.get_barrier_semaphore()
    plane = NY * mp_size

    def z_peer(apart, other):
        return (y * NZ + (z + apart) % NZ, x * NC + (core + other) % NC)

    def plane_peer(far_y, far_x, other):
        return ((y + far_y) % NY) * NZ + z, ((x + far_x) % nx) * NC + (core + other) % NC

    def along_z(semaphore, steps, cores):
        for apart in steps:
            for way in (apart, NZ - apart):
                for other in range(cores):
                    pl.semaphore_signal(semaphore, inc=1, device_id=z_peer(way, other), device_id_type=MESH)

    for apart in range(1, mp_size):
        pl.semaphore_signal(barrier, inc=1, device_id=(dp, (mp + apart) % mp_size), device_id_type=MESH)
    for apart in range(1, NY):
        there = ((y + apart) % NY) * NZ + z
        pl.semaphore_signal(barrier, inc=1, device_id=(there, mp), device_id_type=MESH)
    along_z(barrier, (1, 2), NC)

    low = lax.broadcasted_iota(jnp.int32, (LEN // 2, 2 * RANK), 1) < RANK
    sibling = (dp, x * NC + 1 - core)

    def swap_of(kind):
        return pltpu.make_async_remote_copy(
            part.at[kind, 1 - core],
            from_core.at[kind],
            core_sem.at[kind, 0],
            core_sem.at[kind, 1],
            device_id=sibling,
            device_id_type=MESH,
        )

    def project(i):
        for copy in blocks[i]:
            copy.wait()
        for r in range(i * ROWS, (i + 1) * ROWS, 32):
            span = pl.ds(r, 32)
            half = 0.5 * gate[span, :].astype(F32)
            act = half + half * jnp.tanh(half)
            lhs[0, span, :] = (hidden_grad[span, :].astype(F32) * act).astype(BF16)
            lhs[1, span, :] = (act * up[span, :].astype(F32)).astype(BF16)
        span = pl.ds(i * ROWS, ROWS)
        return [jnp.dot(lhs[j, span, :], hidden[...], preferred_element_type=F32) for j in range(2)]

    weights.wait()
    upward_1, downward_1 = project(0)
    for copy in side:
        copy.wait()
    inward = jnp.dot(tokens[...], model[...], preferred_element_type=F32)
    outward = jnp.dot(out_grad[...], model[...], preferred_element_type=F32)
    part[0, 0] = jnp.where(low, inward[: LEN // 2], pltpu.roll(inward[LEN // 2 :], RANK, 1))
    part[0, 1] = jnp.where(low, pltpu.roll(outward[: LEN // 2], RANK, 1), outward[LEN // 2 :])
    pl.semaphore_wait(barrier, mp_size - 1 + NY - 1 + 4 * NC)
    swap_side = swap_of(0)
    swap_side.start()
    along_z(far_sem.at[0], (2,), 1)
    upward_2, downward_2 = project(1)
    part[1, 0] = jnp.where(low, upward_1, pltpu.roll(upward_2, RANK, 1))
    part[1, 1] = jnp.where(low, pltpu.roll(downward_1, RANK, 1), downward_2)
    swap_hidden = swap_of(1)
    swap_hidden.start()

    def exchange(kind, swap):
        swap.wait_recv()
        xbuf[kind, x] = part[kind, core] + from_core[kind]
        for apart in farthest_first(nx):
            pltpu.make_async_remote_copy(
                xbuf.at[kind, x],
                xbuf.at[kind, x],
                x_sem.at[kind, 0],
                x_sem.at[kind, 1],
                device_id=(dp, ((x + apart) % nx) * NC + core),
                device_id_type=MESH,
            ).start()
        return pltpu.make_async_remote_copy(
            xbuf.at[kind, pl.ds(0, nx - 1)],
            xbuf.at[kind, pl.ds(0, nx - 1)],
            x_sem.at[kind, 0],
            x_sem.at[kind, 1],
            device_id=sibling,
            device_id_type=MESH,
        )

    all_side = exchange(0, swap_side)
    all_hidden = exchange(1, swap_hidden)

    pl.semaphore_wait(far_sem.at[0], 2)
    along_z(far_sem.at[1], (4,), 1)
    all_side.wait_recv()
    side_sum = xbuf[0, 0]
    for i in range(1, nx):
        side_sum = side_sum + xbuf[0, i]
    all_hidden.wait_recv()
    hidden_sum = xbuf[1, 0]
    for i in range(1, nx):
        hidden_sum = hidden_sum + xbuf[1, i]

    left = jnp.where(core == 0, hidden_sum, side_sum)
    right = jnp.where(core == 0, side_sum, hidden_sum)
    both = product_3(left, right)
    diagonal = jnp.where(low, both[:RANK], both[RANK:])
    twice = diagonal + pltpu.roll(diagonal, RANK, 1)
    mbuf[core] = twice
    give = pltpu.make_async_remote_copy(
        mbuf.at[core], mbuf.at[core], m_sem.at[0], m_sem.at[1], device_id=sibling, device_id_type=MESH
    )
    give.start()

    short_lane = lax.broadcasted_iota(jnp.int32, (RANK, 2 * RANK), 1)
    block = jnp.where(low, twice, 0.0)
    gram = product_6(block, jnp.concatenate([block, block], axis=0))
    half_low = lax.broadcasted_iota(jnp.int32, (RANK // 2, 2 * RANK), 1) < RANK
    pairs = jnp.where(half_low, gram[: RANK // 2], gram[RANK // 2 :])
    size = packed.shape[1]
    for i in range(mp_size):
        packed[i] = pairs[i * size : (i + 1) * size]

    pl.semaphore_wait(far_sem.at[1], 2)
    slot = z * NC + core
    for apart in farthest_first(NZ):
        for other in range(NC):
            pltpu.make_async_remote_copy(
                packed.at[x * NC + (core + other) % NC],
                zbuf.at[slot],
                z_sem.at[0],
                z_sem.at[1],
                device_id=z_peer(apart, other),
                device_id_type=MESH,
            ).start()
    pltpu.make_async_remote_copy(
        packed.at[x * NC + 1 - core],
        zbuf.at[slot],
        z_sem.at[0],
        z_sem.at[1],
        device_id=sibling,
        device_id_type=MESH,
    ).start()
    zbuf[slot] = packed[mp]
    give.wait_recv()
    stacked = jnp.where(short_lane < RANK, mbuf[0], mbuf[1])
    own = pltpu.roll(stacked, (RANK + 2 * RANK - mp * (2 * RANK // mp_size)) % (2 * RANK), 1)
    all_z = pltpu.make_async_remote_copy(
        zbuf.at[pl.ds(0, NC * NZ - 1)],
        zbuf.at[pl.ds(0, NC * NZ - 1)],
        z_sem.at[0],
        z_sem.at[1],
        device_id=sibling,
        device_id_type=MESH,
    )
    all_z.wait_recv()
    terms = [zbuf[i] for i in range(NC * NZ)]
    while len(terms) > 1:
        terms = [first + second for first, second in zip(terms[::2], terms[1::2])]
    slice_sum = terms[0]
    place = y * mp_size + mp
    fbuf[place] = slice_sum

    others = [(i, j, k) for i in range(NY) for j in range(nx) for k in range(NC)][1:]
    for far in sorted(others, key=lambda far: -hops(far[0], NY) - hops(far[1], nx)):
        pltpu.make_async_remote_copy(
            fbuf.at[place], fbuf.at[place], f_sem.at[0], f_sem.at[1], device_id=plane_peer(*far), device_id_type=MESH
        ).start()
    all_plane = pltpu.make_async_remote_copy(
        fbuf.at[pl.ds(0, plane - 1)],
        fbuf.at[pl.ds(0, plane - 1)],
        f_sem.at[0],
        f_sem.at[1],
        device_id=sibling,
        device_id_type=MESH,
    )
    all_plane.wait_recv()
    for i in range(mp_size):
        piece = fbuf[i]
        for j in range(1, NY):
            piece = piece + fbuf[j * mp_size + i]
        aug[i * size : (i + 1) * size, :] = piece
    folded = aug[...]
    whole = jnp.concatenate([folded, pltpu.roll(folded, RANK, 1)], axis=0)
    table = jnp.where(short_lane < RANK, whole, own)

    eliminate(table, rows_out)
    factor = math.sqrt(NY * NZ * LEN)
    turned_out = rows_out[...].T
    out_ref[0] = turned_out[RANK : RANK + 2 * RANK // mp_size, :RANK] * factor

    for sent in (swap_side, swap_hidden, all_side, all_hidden, give, all_z, all_plane):
        sent.wait_send()

def shards(tokens_in, gate_pre, up_pre, hidden_grad, out_grad, proj_model, proj_hidden):
    mp_size = lax.axis_size("mp")
    length, width = tokens_in.shape
    units = gate_pre.shape[1]
    ranks = 2 * RANK
    size = RANK * RANK // (mp_size * ranks)
    any_space = pl.BlockSpec(memory_space=pl.ANY)
    return pl.pallas_call(
        functools.partial(kernel, mp_size),
        out_shape=pltpu.VMEM((1, ranks // mp_size, RANK), F32),
        in_specs=[any_space] * 7,
        out_specs=pl.BlockSpec(memory_space=pltpu.VMEM),
        scratch_shapes=[
            pltpu.VMEM((length, width), BF16),
            pltpu.VMEM((length, units), BF16),
            pltpu.VMEM((length, units), BF16),
            pltpu.VMEM((length, units), BF16),
            pltpu.VMEM((length, width), BF16),
            pltpu.VMEM((width, ranks), BF16),
            pltpu.VMEM((units, ranks), BF16),
            pltpu.VMEM((2, length, units), BF16),
            pltpu.VMEM((2, NC, length // 2, ranks), F32),
            pltpu.VMEM((2, length // 2, ranks), F32),
            pltpu.VMEM((2, mp_size // NC, length // 2, ranks), F32),
            pltpu.VMEM((2, RANK, ranks), F32),
            pltpu.VMEM((mp_size, size, ranks), F32),
            pltpu.VMEM((NC * NZ, size, ranks), F32),
            pltpu.VMEM((NY * mp_size, size, ranks), F32),
            pltpu.VMEM((RANK // 2, ranks), F32),
            pltpu.VMEM((ranks, ranks), F32),
            pltpu.SemaphoreType.DMA((4,)),
            pltpu.SemaphoreType.DMA((LEN // ROWS, 3)),
            pltpu.SemaphoreType.DMA((2, 2)),
            pltpu.SemaphoreType.DMA((2, 2)),
            pltpu.SemaphoreType.DMA((2,)),
            pltpu.SemaphoreType.DMA((2,)),
            pltpu.SemaphoreType.DMA((2,)),
            pltpu.SemaphoreType.REGULAR((2,)),
        ],
        compiler_params=pltpu.CompilerParams(collective_id=0, has_side_effects=True),
        name="whiten",
    )(tokens_in, gate_pre, up_pre, hidden_grad, out_grad, proj_model, proj_hidden)


def solution(mesh):
    in_specs = (
        P("dp", "mp"),
        P("dp", "mp"),
        P("dp", "mp"),
        P("dp", "mp"),
        P("dp", "mp"),
        P("mp", None),
        P("mp", None),
    )
    out_specs = P("dp", "mp", None)
    return jax.shard_map(shards, mesh=mesh, in_specs=in_specs, out_specs=out_specs, check_vma=False)
```

```python
import functools
import math

import jax
import jax.numpy as jnp
from jax import lax
from jax.experimental import pallas as pl
from jax.experimental.pallas import tpu as pltpu
from jax.sharding import PartitionSpec as P

RANK = 64
LEN = 128
NY, NZ = 4, 16
NC = 2
ROWS = 64
F32 = jnp.float32
BF16 = jnp.bfloat16
MESH = pl.DeviceIdType.MESH
NT = (((1,), (1,)), ((), ()))
TN = (((0,), (0,)), ((), ()))


def hops(apart, size):
    return min(apart, size - apart)


def farthest_first(size):
    return sorted(range(1, size), key=lambda apart: -hops(apart, size))


def halves(value):
    high = value.astype(BF16)
    return high, (value - high.astype(F32)).astype(BF16)


def thirds(value):
    high = value.astype(BF16)
    rest = value - high.astype(F32)
    mid = rest.astype(BF16)
    return high, mid, (rest - mid.astype(F32)).astype(BF16)


def product_3(left, right):
    lh, ll = halves(left)
    rh, rl = halves(right)
    return lax.dot_general(
        jnp.concatenate([lh, lh, ll], axis=0),
        jnp.concatenate([rh, rl, rh], axis=0),
        TN,
        preferred_element_type=F32,
    )


def product_6(left, right):
    lh, lm, ll = thirds(left)
    rh, rm, rl = thirds(right)
    return lax.dot_general(
        jnp.concatenate([ll, lm, lh, lm, lh, lh], axis=1),
        jnp.concatenate([rh, rm, rl, rh, rm, rh], axis=1),
        NT,
        preferred_element_type=F32,
    )


def eliminate(table, rows_out):
    width = table.shape[1]
    tiles = [table[i : i + 8] for i in range(0, RANK, 8)]
    for t in range(RANK // 8):
        columns = [
            [jnp.broadcast_to(tile[:, 8 * t + j : 8 * t + j + 1], tile.shape) for tile in tiles[t:]] for j in range(8)
        ]
        rows = [jnp.broadcast_to(tiles[t][j : j + 1], (8, width)) for j in range(8)]
        pivot = [[jnp.broadcast_to(columns[j][0][i : i + 1], (8, width)) for j in range(i + 1)] for i in range(8)]
        scaled = []
        for j in range(8):
            inverse = 1.0 / pivot[j][j]
            rows_out[8 * t + j : 8 * t + j + 1, :] = (rows[j] * lax.rsqrt(pivot[j][j]))[:1]
            for m in range(j + 1, 8):
                share = pivot[m][j] * inverse
                rows[m] = rows[m] - share * rows[j]
                for n in range(j + 1, m + 1):
                    pivot[m][n] = pivot[m][n] - share * pivot[n][j]
                columns[m] = [late - share * early for late, early in zip(columns[m], columns[j])]
            scaled.append(rows[j] * inverse)
        for i in range(t + 1, RANK // 8):
            for j in range(8):
                tiles[i] = tiles[i] - columns[j][i - t] * scaled[j]


def kernel(
    mp_size,
    tokens_hbm,
    gate_hbm,
    up_hbm,
    hidden_grad_hbm,
    out_grad_hbm,
    model_hbm,
    hidden_hbm,
    out_ref,
    tokens,
    gate,
    up,
    hidden_grad,
    out_grad,
    model,
    hidden,
    lhs,
    part,
    from_core,
    xbuf,
    mbuf,
    packed,
    zbuf,
    fbuf,
    aug,
    rows_out,
    in_sem,
    block_sem,
    core_sem,
    x_sem,
    m_sem,
    z_sem,
    f_sem,
    far_sem,
):
    nx = mp_size // NC
    dp = lax.axis_index("dp")
    mp = lax.axis_index("mp")
    y, z = dp // NZ, dp % NZ
    x, core = mp // NC, mp % NC

    weights = pltpu.make_async_copy(hidden_hbm, hidden, in_sem.at[0])
    side = [
        pltpu.make_async_copy(model_hbm, model, in_sem.at[1]),
        pltpu.make_async_copy(tokens_hbm, tokens, in_sem.at[2]),
        pltpu.make_async_copy(out_grad_hbm, out_grad, in_sem.at[3]),
    ]
    weights.start()
    blocks = []
    for i in range(LEN // ROWS):
        span = pl.ds(i * ROWS, ROWS)
        group = [
            pltpu.make_async_copy(gate_hbm.at[span, :], gate.at[span, :], block_sem.at[i, 0]),
            pltpu.make_async_copy(hidden_grad_hbm.at[span, :], hidden_grad.at[span, :], block_sem.at[i, 1]),
            pltpu.make_async_copy(up_hbm.at[span, :], up.at[span, :], block_sem.at[i, 2]),
        ]
        blocks.append(group)
    for copy in blocks[0] + side + blocks[1]:
        copy.start()

    barrier = pltpu.get_barrier_semaphore()
    plane = NY * mp_size

    def z_peer(apart, other):
        return (y * NZ + (z + apart) % NZ, x * NC + (core + other) % NC)

    def plane_peer(far_y, far_x, other):
        return ((y + far_y) % NY) * NZ + z, ((x + far_x) % nx) * NC + (core + other) % NC

    def along_z(semaphore, steps, cores):
        for apart in steps:
            for way in (apart, NZ - apart):
                for other in range(cores):
                    pl.semaphore_signal(semaphore, inc=1, device_id=z_peer(way, other), device_id_type=MESH)

    for apart in range(1, mp_size):
        pl.semaphore_signal(barrier, inc=1, device_id=(dp, (mp + apart) % mp_size), device_id_type=MESH)
    for apart in range(1, NY):
        there = ((y + apart) % NY) * NZ + z
        pl.semaphore_signal(barrier, inc=1, device_id=(there, mp), device_id_type=MESH)
    along_z(barrier, (1, 2), NC)

    low = lax.broadcasted_iota(jnp.int32, (LEN // 2, 2 * RANK), 1) < RANK
    sibling = (dp, x * NC + 1 - core)

    def swap_of(kind):
        return pltpu.make_async_remote_copy(
            part.at[kind, 1 - core],
            from_core.at[kind],
            core_sem.at[kind, 0],
            core_sem.at[kind, 1],
            device_id=sibling,
            device_id_type=MESH,
        )

    def weigh(i):
        for copy in blocks[i]:
            copy.wait()
        for r in range(i * ROWS, (i + 1) * ROWS, 32):
            span = pl.ds(r, 32)
            half = 0.5 * gate[span, :].astype(F32)
            act = half + half * jnp.tanh(half)
            lhs[0, span, :] = (hidden_grad[span, :].astype(F32) * act).astype(BF16)
            lhs[1, span, :] = (act * up[span, :].astype(F32)).astype(BF16)

    def project(i, j):
        return jnp.dot(lhs[j, pl.ds(i * ROWS, ROWS), :], hidden[...], preferred_element_type=F32)

    def exchange(kind, swap):
        swap.wait_recv()
        xbuf[kind, x] = part[kind, core] + from_core[kind]
        for apart in farthest_first(nx):
            pltpu.make_async_remote_copy(
                xbuf.at[kind, x],
                xbuf.at[kind, x],
                x_sem.at[kind, 0],
                x_sem.at[kind, 1],
                device_id=(dp, ((x + apart) % nx) * NC + core),
                device_id_type=MESH,
            ).start()
        return pltpu.make_async_remote_copy(
            xbuf.at[kind, pl.ds(0, nx - 1)],
            xbuf.at[kind, pl.ds(0, nx - 1)],
            x_sem.at[kind, 0],
            x_sem.at[kind, 1],
            device_id=sibling,
            device_id_type=MESH,
        )

    weights.wait()
    weigh(0)
    upward_1, downward_1 = project(0, 0), project(0, 1)
    for copy in side:
        copy.wait()
    inward = jnp.dot(tokens[...], model[...], preferred_element_type=F32)
    outward = jnp.dot(out_grad[...], model[...], preferred_element_type=F32)
    part[0, 0] = jnp.where(low, inward[: LEN // 2], pltpu.roll(inward[LEN // 2 :], RANK, 1))
    part[0, 1] = jnp.where(low, pltpu.roll(outward[: LEN // 2], RANK, 1), outward[LEN // 2 :])
    pl.semaphore_wait(barrier, mp_size - 1 + NY - 1 + 4 * NC)
    swap_side = swap_of(0)
    swap_side.start()
    along_z(far_sem.at[0], (2,), 1)
    weigh(1)
    upward_2 = project(1, 0)
    all_side = exchange(0, swap_side)
    downward_2 = project(1, 1)
    part[1, 0] = jnp.where(low, upward_1, pltpu.roll(upward_2, RANK, 1))
    part[1, 1] = jnp.where(low, pltpu.roll(downward_1, RANK, 1), downward_2)
    swap_hidden = swap_of(1)
    swap_hidden.start()

    all_hidden = exchange(1, swap_hidden)

    pl.semaphore_wait(far_sem.at[0], 2)
    along_z(far_sem.at[1], (4,), 1)
    all_side.wait_recv()
    side_sum = xbuf[0, 0]
    for i in range(1, nx):
        side_sum = side_sum + xbuf[0, i]
    all_hidden.wait_recv()
    hidden_sum = xbuf[1, 0]
    for i in range(1, nx):
        hidden_sum = hidden_sum + xbuf[1, i]

    left = jnp.where(core == 0, hidden_sum, side_sum)
    right = jnp.where(core == 0, side_sum, hidden_sum)
    both = product_3(left, right)
    diagonal = jnp.where(low, both[:RANK], both[RANK:])
    twice = diagonal + pltpu.roll(diagonal, RANK, 1)
    mbuf[core] = twice
    give = pltpu.make_async_remote_copy(
        mbuf.at[core], mbuf.at[core], m_sem.at[0], m_sem.at[1], device_id=sibling, device_id_type=MESH
    )
    give.start()

    short_lane = lax.broadcasted_iota(jnp.int32, (RANK, 2 * RANK), 1)
    block = jnp.where(low, twice, 0.0)
    gram = product_6(block, jnp.concatenate([block, block], axis=0))
    half_low = lax.broadcasted_iota(jnp.int32, (RANK // 2, 2 * RANK), 1) < RANK
    pairs = jnp.where(half_low, gram[: RANK // 2], gram[RANK // 2 :])
    size = packed.shape[1]
    for i in range(mp_size):
        packed[i] = pairs[i * size : (i + 1) * size]

    pl.semaphore_wait(far_sem.at[1], 2)
    slot = z * NC + core
    for apart in farthest_first(NZ):
        for other in range(NC):
            pltpu.make_async_remote_copy(
                packed.at[x * NC + (core + other) % NC],
                zbuf.at[slot],
                z_sem.at[0],
                z_sem.at[1],
                device_id=z_peer(apart, other),
                device_id_type=MESH,
            ).start()
    pltpu.make_async_remote_copy(
        packed.at[x * NC + 1 - core],
        zbuf.at[slot],
        z_sem.at[0],
        z_sem.at[1],
        device_id=sibling,
        device_id_type=MESH,
    ).start()
    zbuf[slot] = packed[mp]
    give.wait_recv()
    stacked = jnp.where(short_lane < RANK, mbuf[0], mbuf[1])
    own = pltpu.roll(stacked, (RANK + 2 * RANK - mp * (2 * RANK // mp_size)) % (2 * RANK), 1)
    all_z = pltpu.make_async_remote_copy(
        zbuf.at[pl.ds(0, NC * NZ - 1)],
        zbuf.at[pl.ds(0, NC * NZ - 1)],
        z_sem.at[0],
        z_sem.at[1],
        device_id=sibling,
        device_id_type=MESH,
    )
    all_z.wait_recv()
    terms = [zbuf[i] for i in range(NC * NZ)]
    while len(terms) > 1:
        terms = [first + second for first, second in zip(terms[::2], terms[1::2])]
    slice_sum = terms[0]
    place = y * mp_size + mp
    fbuf[place] = slice_sum

    others = [(i, j, k) for i in range(NY) for j in range(nx) for k in range(NC)][1:]
    for far in sorted(others, key=lambda far: -hops(far[0], NY) - hops(far[1], nx)):
        pltpu.make_async_remote_copy(
            fbuf.at[place], fbuf.at[place], f_sem.at[0], f_sem.at[1], device_id=plane_peer(*far), device_id_type=MESH
        ).start()
    all_plane = pltpu.make_async_remote_copy(
        fbuf.at[pl.ds(0, plane - 1)],
        fbuf.at[pl.ds(0, plane - 1)],
        f_sem.at[0],
        f_sem.at[1],
        device_id=sibling,
        device_id_type=MESH,
    )
    all_plane.wait_recv()
    for i in range(mp_size):
        piece = fbuf[i]
        for j in range(1, NY):
            piece = piece + fbuf[j * mp_size + i]
        aug[i * size : (i + 1) * size, :] = piece
    folded = aug[...]
    whole = jnp.concatenate([folded, pltpu.roll(folded, RANK, 1)], axis=0)
    table = jnp.where(short_lane < RANK, whole, own)

    eliminate(table, rows_out)
    factor = math.sqrt(NY * NZ * LEN)
    turned_out = rows_out[...].T
    out_ref[0] = turned_out[RANK : RANK + 2 * RANK // mp_size, :RANK] * factor

    for sent in (swap_side, swap_hidden, all_side, all_hidden, give, all_z, all_plane):
        sent.wait_send()

def shards(tokens_in, gate_pre, up_pre, hidden_grad, out_grad, proj_model, proj_hidden):
    mp_size = lax.axis_size("mp")
    length, width = tokens_in.shape
    units = gate_pre.shape[1]
    ranks = 2 * RANK
    size = RANK * RANK // (mp_size * ranks)
    any_space = pl.BlockSpec(memory_space=pl.ANY)
    return pl.pallas_call(
        functools.partial(kernel, mp_size),
        out_shape=pltpu.VMEM((1, ranks // mp_size, RANK), F32),
        in_specs=[any_space] * 7,
        out_specs=pl.BlockSpec(memory_space=pltpu.VMEM),
        scratch_shapes=[
            pltpu.VMEM((length, width), BF16),
            pltpu.VMEM((length, units), BF16),
            pltpu.VMEM((length, units), BF16),
            pltpu.VMEM((length, units), BF16),
            pltpu.VMEM((length, width), BF16),
            pltpu.VMEM((width, ranks), BF16),
            pltpu.VMEM((units, ranks), BF16),
            pltpu.VMEM((2, length, units), BF16),
            pltpu.VMEM((2, NC, length // 2, ranks), F32),
            pltpu.VMEM((2, length // 2, ranks), F32),
            pltpu.VMEM((2, mp_size // NC, length // 2, ranks), F32),
            pltpu.VMEM((2, RANK, ranks), F32),
            pltpu.VMEM((mp_size, size, ranks), F32),
            pltpu.VMEM((NC * NZ, size, ranks), F32),
            pltpu.VMEM((NY * mp_size, size, ranks), F32),
            pltpu.VMEM((RANK // 2, ranks), F32),
            pltpu.VMEM((ranks, ranks), F32),
            pltpu.SemaphoreType.DMA((4,)),
            pltpu.SemaphoreType.DMA((LEN // ROWS, 3)),
            pltpu.SemaphoreType.DMA((2, 2)),
            pltpu.SemaphoreType.DMA((2, 2)),
            pltpu.SemaphoreType.DMA((2,)),
            pltpu.SemaphoreType.DMA((2,)),
            pltpu.SemaphoreType.DMA((2,)),
            pltpu.SemaphoreType.REGULAR((2,)),
        ],
        compiler_params=pltpu.CompilerParams(collective_id=0, has_side_effects=True),
        name="whiten",
    )(tokens_in, gate_pre, up_pre, hidden_grad, out_grad, proj_model, proj_hidden)


def solution(mesh):
    in_specs = (
        P("dp", "mp"),
        P("dp", "mp"),
        P("dp", "mp"),
        P("dp", "mp"),
        P("dp", "mp"),
        P("mp", None),
        P("mp", None),
    )
    out_specs = P("dp", "mp", None)
    return jax.shard_map(shards, mesh=mesh, in_specs=in_specs, out_specs=out_specs, check_vma=False)
```
